128 devices in a mesh: blk: 2 (over z_hi), row: 64 (over x, z_lo, y, core).
Axes of the slice: x: 4, y: 4, z: 4 (z_hi: 2, z_lo: 2; z = z_hi * 2 + z_lo), core: 2. Of those that a mesh axis runs over, the one named last changes fastest.
Arguments:
- features: bfloat16 [65536, 128], P(('blk', 'row')), may hold values from -6 to 6
- tiles: bfloat16 [512, 32, 128, 128], P(('blk', 'row')), may hold values from -0.75 to 0.75
- tile_src: int32 [512, 32], P(('blk', 'row')), may hold values from 0 to 511, as said below
- tile_count: int32 [512], P(('blk', 'row')), may hold values from 1 to 32, 8448 in all
- degrees: int32 [65536], P(('blk', 'row')), may hold values from 16 to 128
- w_self: bfloat16 [128, 128], replicated, may hold values from -0.5 to 0.5
- w_neigh: bfloat16 [128, 128], replicated, may hold values from -2 to 2
- bias: float32 [128], replicated, may hold values from -3 to 3
Outputs:
- updated: bfloat16 [65536, 128], P(('blk', 'row'))
The draws below stay inside these ranges and needn't reach their ends.
Inputs may be any that keep to these rules, and one draw needn't show every extreme that they name: `tile_src`: slots at or past tile_count of a block are unused; their tiles are arbitrary. Split the node blocks into aligned runs of 4 blocks and the destination blocks likewise: all slots of the destination blocks of one run name at most one source block of each run of source blocks.
All inputs are finite; a program needn't handle non-finite values.
Results may differ from the reference program's by a relative error of at most 0.0028.
Values may be sent and summed in bfloat16 or wider, within the bound.
A program may use at most 128 MiB of HBM per device.

```python
import math
import jax
import jax.numpy as jnp
import numpy as np
from jax import lax

F = 128
TILE = 128
TPB = 32
NODE_DEV = 512
NODES = 65536
NB = 512


def draw_tile_src(key, part):
    held = NODE_DEV // TILE
    owners = NB // held
    chosen = jax.random.randint(jax.random.fold_in(key, 11), (owners, owners), 0, held)
    owner = jax.random.randint(jax.random.fold_in(key, 12), (NB, TPB), 0, owners)
    rows = chosen[jnp.arange(NB, dtype=jnp.int32) // held]
    local = jnp.take_along_axis(rows, owner, axis=1)
    return (owner * held + local).astype(jnp.int32)


def place_ends(array, rng, least, largest):
    shape = array.shape
    spot = [jax.random.randint(jax.random.fold_in(rng, axis), (), 0, shape[axis]) for axis in range(len(shape))]
    array = array.at[tuple(spot)].set(least)
    longest = shape.index(max(shape))
    spot[longest] = (spot[longest] + 1) % shape[longest]
    return array.at[tuple(spot)].set(largest)


def level_of(rng, shape, shards, least, high):
    loudness = 1.0
    for axis_at, blocks in shards:
        draws = jax.random.uniform(jax.random.fold_in(jax.random.fold_in(rng, 6), axis_at), (blocks,), jnp.float32, least / len(shards), high / len(shards))
        loudness = loudness * jnp.repeat(jnp.exp(draws), shape[axis_at] // blocks).reshape((-1,) + (1,) * (len(shape) - 1 - axis_at))
    return loudness


def profile(count, total, limit, skew):
    loads = [(1 << 20) // math.isqrt(rank ** skew) + 1 for rank in range(2, count + 1)]
    spare, given = total - limit - (count - 1), [1] * (count - 1)
    while spare > 0:
        candidates = [i for i in range(count - 1) if given[i] < limit]
        pool, budget = sum([loads[i] for i in candidates]), spare
        for i in candidates:
            extra = min(limit - given[i], max(1, budget * loads[i] // pool), spare)
            given[i] = given[i] + extra
            spare = spare - extra
    return np.array([limit] + given)


def ragged(stream_key, number_of, total, most, slope):
    if number_of == 2:
        one = jax.random.randint(stream_key, (), max(1, total - most), min(most, total - 1) + 1)
        return jnp.stack([one, total - one])
    sizes = jnp.asarray(profile(number_of, total, most, slope), jnp.int32)
    couples = (number_of - 1) // 2
    donor, receiver = sizes[1:1 + 2 * couples:2], sizes[2:2 + 2 * couples:2]
    slack = jnp.minimum(donor - 1, most - receiver)
    shifted = jax.random.randint(jax.random.fold_in(stream_key, 1), (couples,), 0, 1 << 20) % (slack + 1)
    sizes = sizes.at[1:1 + 2 * couples:2].set(donor - shifted).at[2:2 + 2 * couples:2].set(receiver + shifted)
    return sizes[jax.random.permutation(jax.random.fold_in(stream_key, 2), number_of)]


def normal_values(rng, extent, spread, bound, cuts=(), kind=jnp.bfloat16):
    values = jax.random.normal(rng, extent, jnp.float32) * spread
    if len(cuts) > 0:
        values = level_of(rng, extent, cuts, -0.22, 0.18) * values
    return jnp.clip(values, min=-bound, max=bound).astype(kind)


def setup_inputs(seed: int = 0) -> dict:
    seeds = jax.random.split(jax.random.key(seed), 9)
    features = normal_values(seeds[0], (NODES, F), 1.0, 6.0, ((0, 128),))
    tiles = normal_values(seeds[1], (NB, TPB, TILE, TILE), 0.125, 0.75, ((0, 128),))
    tile_src = draw_tile_src(jax.random.fold_in(seeds[8], 71), 0)
    tile_count = ragged(seeds[3], NB, NB + NB * (TPB - 1) // 2, TPB, 2).astype(jnp.int32)
    degrees = place_ends(jax.random.randint(seeds[4], (NODES,), 16, 129), jax.random.fold_in(seeds[4], 1), 16, 128).astype(jnp.int32)
    w_self = normal_values(seeds[5], (F, F), F ** -0.5, 0.5)
    w_neigh = normal_values(seeds[6], (F, F), (F // 16) ** -0.5, 2.0)
    bias = normal_values(seeds[7], (F,), 0.5, 3.0, (), jnp.float32)
    return {"features": features, "tiles": tiles, "tile_src": tile_src, "tile_count": tile_count, "degrees": degrees, "w_self": w_self, "w_neigh": w_neigh, "bias": bias}


def reference(features, tiles, tile_src, tile_count, degrees, w_self, w_neigh, bias):
    blocks = features.reshape(NB, TILE, F)
    slot_ids = jnp.arange(TPB, dtype=jnp.int32)

    def one_block(item):
        tile_row, src_row, count = item
        sources = blocks[src_row].astype(jnp.float32)
        live = (slot_ids < count).astype(jnp.float32)
        sources = sources * live[:, None, None]
        return jnp.einsum("tij,tjf->if", tile_row.astype(jnp.float32), sources)

    aggregate = lax.map(one_block, (tiles, tile_src, tile_count)).reshape(NODES, F)
    neigh_mean = (aggregate / degrees.astype(jnp.float32)[:, None]).astype(jnp.bfloat16)
    total = jnp.dot(features, w_self, preferred_element_type=jnp.float32)
    total = total + jnp.dot(neigh_mean, w_neigh, preferred_element_type=jnp.float32)
    return jax.nn.relu(total + bias[None, :]).astype(jnp.bfloat16)
```

```python
import jax
import jax.numpy as jnp
from jax import lax
from jax.experimental import pallas as pl
from jax.experimental.pallas import tpu as pltpu
from jax.sharding import PartitionSpec as P

MESH = pl.DeviceIdType.MESH
SPLITS = ((0, 48), (48, 48), (96, 32))
ORDERS = ((0, 1, 2), (1, 2, 0), (2, 0, 1))


def place():
    group, member = lax.axis_index("blk"), lax.axis_index("row")
    x = lax.div(member, 16)
    z_low = lax.rem(lax.div(member, 8), 2)
    y = lax.rem(lax.div(member, 2), 4)
    return [x, y, group * 2 + z_low], lax.rem(member, 2)


def device(spot, core):
    x, y, z = spot
    return lax.div(z, 2), ((x * 2 + lax.rem(z, 2)) * 4 + y) * 2 + core


def shifted(spot, axis, steps):
    moved = list(spot)
    moved[axis] = lax.rem(moved[axis] + steps, 4)
    return moved


def exchange_kernel(feat, tiles, src, cnt, out0, out1, out2, tiles_out, *scratch):
    outs = (out0, out1, out2)
    held = (scratch[0:4], scratch[4:8], scratch[8:12])
    packs, relays = scratch[12:15], scratch[15:18]
    mine, table, wants = scratch[18:21]
    load_sem, tile_sem, one_recv, two_recv, held_send = scratch[21:26]
    want_send, want_recv, want_local, pack_send, out_recv, relay_recv, relay_send = scratch[26:33]

    spot, core = place()
    other = 1 - core

    loads = []
    for k, (start, rows) in enumerate(SPLITS):
        copy = pltpu.make_async_copy(feat.at[:, pl.ds(start, rows), :], held[k][0].at[0], load_sem.at[k])
        copy.start()
        loads.append(copy)
    tile_load = pltpu.make_async_copy(tiles, tiles_out, tile_sem)

    friends = [device(spot, other)]
    for axis in range(3):
        for steps in (1, 2, 3):
            for c in (core, other):
                friends.append(device(shifted(spot, axis, steps), c))
    barrier = pltpu.get_barrier_semaphore()
    for friend in friends:
        pl.semaphore_signal(barrier, inc=1, device_id=friend, device_id_type=MESH)
    pl.semaphore_wait(barrier, len(friends))

    def send(source, target, send_sem, recv_sem, where):
        copy = pltpu.make_async_remote_copy(
            src_ref=source, dst_ref=target, send_sem=send_sem, recv_sem=recv_sem,
            device_id=where, device_id_type=MESH,
        )
        copy.start()

    def arrived(ref, sem):
        pltpu.make_async_copy(ref, ref, sem).wait()

    plus = [device(shifted(spot, axis, 1), core) for axis in range(3)]
    minus = [device(shifted(spot, axis, 3), core) for axis in range(3)]
    plus_other = [device(shifted(spot, axis, 1), other) for axis in range(3)]
    minus_other = [device(shifted(spot, axis, 3), other) for axis in range(3)]

    def spread(k, d1):
        a2 = ORDERS[k][1]
        own = held[k][0].at[d1]
        send(own, held[k][3].at[d1], held_send.at[k], two_recv.at[k, d1, 0], plus[a2])
        send(own, held[k][1].at[d1], held_send.at[k], two_recv.at[k, d1, 1], minus[a2])

    def spread_on(k, d1):
        a2 = ORDERS[k][1]
        arrived(held[k][3].at[d1], two_recv.at[k, d1, 0])
        send(held[k][3].at[d1, 0:2], held[k][2].at[d1, 0:2], held_send.at[k], two_recv.at[k, d1, 2], plus[a2])
        arrived(held[k][1].at[d1], two_recv.at[k, d1, 1])
        send(held[k][1].at[d1, 2:4], held[k][2].at[d1, 2:4], held_send.at[k], two_recv.at[k, d1, 3], minus[a2])

    def select(k, d2):
        a1, a2, a3 = ORDERS[k]
        for d1 in range(4):
            group, member = device(shifted(shifted(spot, a1, d1), a2, d2), core)
            lane = group * 64 + member
            for j in range(8):
                row = j if j < 2 else 2 + k * 6 + (j - 2)
                block = held[k][d2][d1, wants[row, 0, lane]]
                if j == 0:
                    outs[k][0, d2, d1] = block
                else:
                    packs[k][j - 1, d2, d1] = block
        send(packs[k].at[0, d2], outs[k].at[1, d2], pack_send.at[k], out_recv.at[k], device(spot, other))
        send(packs[k].at[3, d2], relays[k].at[0, d2], pack_send.at[k], relay_recv.at[k, 0, d2], plus[a3])
        send(packs[k].at[4, d2], relays[k].at[1, d2], pack_send.at[k], relay_recv.at[k, 1, d2], minus[a3])
        send(packs[k].at[1, d2], outs[k].at[6, d2], pack_send.at[k], out_recv.at[k], plus[a3])
        send(packs[k].at[5, d2], outs[k].at[2, d2], pack_send.at[k], out_recv.at[k], minus[a3])
        send(packs[k].at[2, d2], outs[k].at[7, d2], pack_send.at[k], out_recv.at[k], plus_other[a3])
        send(packs[k].at[6, d2], outs[k].at[3, d2], pack_send.at[k], out_recv.at[k], minus_other[a3])

    def relay(k, d2):
        a3 = ORDERS[k][2]
        arrived(relays[k].at[0, d2], relay_recv.at[k, 0, d2])
        send(relays[k].at[0, d2], outs[k].at[4, d2], relay_send.at[k], out_recv.at[k], plus[a3])
        arrived(relays[k].at[1, d2], relay_recv.at[k, 1, d2])
        send(relays[k].at[1, d2], outs[k].at[5, d2], relay_send.at[k], out_recv.at[k], minus_other[a3])

    for k in range(3):
        loads[k].wait()
        a1 = ORDERS[k][0]
        own = held[k][0].at[0]
        send(own, held[k][0].at[3], held_send.at[k], one_recv.at[k, 0], plus[a1])
        send(own, held[k][0].at[1], held_send.at[k], one_recv.at[k, 1], minus[a1])
        spread(k, 0)
    tile_load.start()

    lanes = lax.broadcasted_iota(jnp.int32, (1, 128), 1)
    want = jnp.zeros((1, 128), jnp.int32)
    for b in range(4):
        for t in range(32):
            block = src[b, t]
            owner = jnp.where(t < cnt[b], lax.shift_right_logical(block, 2), -1)
            want = jnp.where(lanes == owner, lax.bitwise_and(block, 3), want)
    mine[...] = want
    send(mine, table.at[0], want_send, want_recv, device(spot, other))
    for k in range(3):
        a3 = ORDERS[k][2]
        for e in (1, 2, 3):
            back = shifted(spot, a3, 4 - e)
            send(mine, table.at[1 + k * 6 + e * 2 - 2], want_send, want_recv, device(back, core))
            send(mine, table.at[1 + k * 6 + e * 2 - 1], want_send, want_recv, device(back, other))

    for k in range(3):
        a1 = ORDERS[k][0]
        arrived(held[k][0].at[3], one_recv.at[k, 0])
        send(held[k][0].at[3, 0:2], held[k][0].at[2, 0:2], held_send.at[k], one_recv.at[k, 2], plus[a1])
        spread(k, 3)
        arrived(held[k][0].at[1], one_recv.at[k, 1])
        send(held[k][0].at[1, 2:4], held[k][0].at[2, 2:4], held_send.at[k], one_recv.at[k, 3], minus[a1])
        spread(k, 1)
    for k in range(3):
        spread_on(k, 0)
    for k in range(3):
        arrived(held[k][0].at[2, 0:2], one_recv.at[k, 2])
        arrived(held[k][0].at[2, 2:4], one_recv.at[k, 3])
        spread(k, 2)

    arrived(table, want_recv)
    own_row = pltpu.make_async_copy(mine, wants.at[0], want_local.at[0])
    others = pltpu.make_async_copy(table, wants.at[pl.ds(1, 19)], want_local.at[1])
    own_row.start()
    others.start()
    own_row.wait()
    others.wait()

    for k in range(3):
        select(k, 0)
        spread_on(k, 3)
        spread_on(k, 1)
    for k in range(3):
        spread_on(k, 2)
        select(k, 3)
        select(k, 1)
        relay(k, 0)
    for k in range(3):
        for d1 in range(4):
            arrived(held[k][2].at[d1, 0:2], two_recv.at[k, d1, 2])
            arrived(held[k][2].at[d1, 2:4], two_recv.at[k, d1, 3])
        select(k, 2)
    for d2 in (3, 1, 2):
        for k in range(3):
            relay(k, d2)

    for k in range(3):
        arrived(outs[k].at[pl.ds(1, 7)], out_recv.at[k])
    arrived(table, want_send)
    for k in range(3):
        arrived(packs[k], pack_send.at[k])
        arrived(relays[k], relay_send.at[k])
        sent = packs[k].at[pl.ds(0, 3), pl.ds(0, 4), pl.ds(0, 4)]
        arrived(sent, held_send.at[k])
        more = packs[k].at[0, pl.ds(0, 3), pl.ds(0, 4)]
        arrived(more, held_send.at[k])
    tile_load.wait()


def exchange(features, tiles, tile_src, tile_count):
    rows = [r for _, r in SPLITS]
    vmem = pl.BlockSpec(memory_space=pltpu.VMEM)
    smem = pl.BlockSpec(memory_space=pltpu.SMEM)
    hbm = pl.BlockSpec(memory_space=pl.ANY)
    dma = pltpu.SemaphoreType.DMA
    scratch = [pltpu.VMEM((4, 4, r, 128), jnp.bfloat16) for r in rows for _ in range(4)]
    scratch += [pltpu.VMEM((7, 4, 4, r, 128), jnp.bfloat16) for r in rows]
    scratch += [pltpu.VMEM((2, 4, 4, r, 128), jnp.bfloat16) for r in rows]
    scratch += [pltpu.VMEM((1, 128), jnp.int32), pltpu.VMEM((19, 1, 128), jnp.int32), pltpu.SMEM((20, 1, 128), jnp.int32)]
    scratch += [dma((3,)), dma, dma((3, 4)), dma((3, 4, 4)), dma((3,))]
    scratch += [dma, dma, dma((2,)), dma((3,)), dma((3,)), dma((3, 2, 4)), dma((3,))]
    shapes = [jax.ShapeDtypeStruct((8, 4, 4, r, 128), jnp.bfloat16) for r in rows]
    shapes.append(jax.ShapeDtypeStruct(tiles.shape, tiles.dtype))
    return pl.pallas_call(
        exchange_kernel,
        out_shape=shapes,
        in_specs=[hbm, hbm, smem, smem],
        out_specs=[vmem] * 4,
        scratch_shapes=scratch,
        compiler_params=pltpu.CompilerParams(collective_id=0, has_side_effects=True, vmem_limit_bytes=60 << 20),
        name="exchange",
    )(features, tiles, tile_src, tile_count)


def combine_kernel(src, cnt, f0, f1, f2, tiles, feat, deg, w_self, w_neigh, bias, out):
    spot, core = place()
    x, y, z = spot

    def one_block(b, carry):
        live = cnt[b]
        total = jnp.zeros((128, 128), jnp.float32)
        for pair in range(16):
            blocks, sides = [], []
            for t in (2 * pair, 2 * pair + 1):
                owner = lax.shift_right_logical(src[b, t], 2)
                rc = lax.bitwise_xor(lax.bitwise_and(owner, 1), core)
                sy = lax.bitwise_and(lax.shift_right_logical(owner, 1), 3)
                sx = lax.bitwise_and(lax.shift_right_logical(owner, 4), 3)
                sz = lax.bitwise_and(lax.shift_right_logical(owner, 3), 1) + 2 * lax.shift_right_logical(owner, 6)
                rx, ry, rz = (lax.bitwise_and(s - m, 3) for s, m in ((sx, x), (sy, y), (sz, z)))
                block = jnp.concatenate([
                    f0[((rz * 2 + rc) * 4 + ry) * 4 + rx],
                    f1[((rx * 2 + rc) * 4 + rz) * 4 + ry],
                    f2[((ry * 2 + rc) * 4 + rx) * 4 + rz],
                ], axis=0)
                blocks.append(jnp.where(t < live, block, jnp.zeros_like(block)))
                sides.append(tiles[b, t])
            total = total + jnp.dot(
                jnp.concatenate(sides, axis=1), jnp.concatenate(blocks, axis=0),
                preferred_element_type=jnp.float32,
            )
        rows = pl.ds(pl.multiple_of(b * 128, 128), 128)
        degrees = jnp.broadcast_to(deg[pl.ds(b, 1), :].astype(jnp.float32), (128, 128)).T
        mean = (total / degrees).astype(jnp.bfloat16)
        summed = jnp.dot(feat[rows, :], w_self[...], preferred_element_type=jnp.float32)
        summed = summed + jnp.dot(mean, w_neigh[...], preferred_element_type=jnp.float32)
        out[rows, :] = jnp.maximum(summed + bias[...], 0.0).astype(jnp.bfloat16)
        return carry

    lax.fori_loop(0, 4, one_block, 0)


def combine(picked, tiles, features, tile_src, tile_count, degrees, w_self, w_neigh, bias):
    vmem = pl.BlockSpec(memory_space=pltpu.VMEM)
    smem = pl.BlockSpec(memory_space=pltpu.SMEM)
    return pl.pallas_call(
        combine_kernel,
        out_shape=jax.ShapeDtypeStruct(features.shape, jnp.bfloat16),
        in_specs=[smem, smem] + [vmem] * 9,
        out_specs=vmem,
        compiler_params=pltpu.CompilerParams(vmem_limit_bytes=60 << 20),
        name="combine",
    )(tile_src, tile_count, *picked, tiles, features, degrees, w_self, w_neigh, bias)


def per_device(features, tiles, tile_src, tile_count, degrees, w_self, w_neigh, bias):
    *picked, held_tiles = exchange(features.reshape(4, 128, 128), tiles, tile_src, tile_count)
    picked = [p.reshape(128, p.shape[3], 128) for p in picked]
    return combine(
        picked, held_tiles, features, tile_src, tile_count,
        degrees.reshape(4, 128), w_self, w_neigh, bias.reshape(1, 128),
    )


def solution(mesh):
    return jax.shard_map(
        per_device,
        mesh=mesh,
        in_specs=(
            P(("blk", "row"), None),
            P(("blk", "row"), None, None, None),
            P(("blk", "row"), None),
            P(("blk", "row")),
            P(("blk", "row")),
            P(),
            P(),
            P(),
        ),
        out_specs=P(("blk", "row"), None),
        check_vma=False,
    )
```

```python
import jax
import jax.numpy as jnp
from jax import lax
from jax.experimental import pallas as pl
from jax.experimental.pallas import tpu as pltpu
from jax.sharding import PartitionSpec as P

MESH = pl.DeviceIdType.MESH
VMEM_BYTES = 66_800_000
SPLITS = ((0, 48), (48, 48), (96, 32))
ORDERS = ((0, 1, 2), (1, 2, 0), (2, 0, 1))


def place():
    group, member = lax.axis_index("blk"), lax.axis_index("row")
    x = lax.div(member, 16)
    z_low = lax.rem(lax.div(member, 8), 2)
    y = lax.rem(lax.div(member, 2), 4)
    return [x, y, group * 2 + z_low], lax.rem(member, 2)


def device(spot, core):
    x, y, z = spot
    return lax.div(z, 2), ((x * 2 + lax.rem(z, 2)) * 4 + y) * 2 + core


def shifted(spot, axis, steps):
    moved = list(spot)
    moved[axis] = lax.rem(moved[axis] + steps, 4)
    return moved


def layer_kernel(feat, tiles, src_hbm, cnt_hbm, deg_hbm, self_hbm, neigh_hbm, bias_hbm, out, *scratch):
    held = (scratch[0:4], scratch[4:8], scratch[8:12])
    packs, relays, outs = scratch[12:15], scratch[15:18], scratch[18:21]
    mine, table, wants, src, cnt, src_vec, spots_vec, spots = scratch[21:29]
    feat_vec, tiles_vec, deg, w_self, w_neigh, bias, base = scratch[29:36]
    load_sem, one_recv, two_recv, held_send = scratch[36:40]
    want_send, want_recv, want_local, pack_send, out_recv, relay_recv, relay_send = scratch[40:47]

    spot, core = place()
    other = 1 - core

    def load(source, target, at):
        copy = pltpu.make_async_copy(source, target, load_sem.at[at])
        copy.start()
        return copy

    loads = [
        load(feat.at[:, pl.ds(start, rows), :], held[k][0].at[0], k)
        for k, (start, rows) in enumerate(SPLITS)
    ]
    table_loads = [load(src_hbm, src, 3), load(cnt_hbm, cnt, 4), load(src_hbm, src_vec, 5)]

    friends = [device(spot, other)]
    for axis in range(3):
        for steps in (1, 2, 3):
            for c in (core, other):
                friends.append(device(shifted(spot, axis, steps), c))
    barrier = pltpu.get_barrier_semaphore()
    for friend in friends:
        pl.semaphore_signal(barrier, inc=1, device_id=friend, device_id_type=MESH)
    pl.semaphore_wait(barrier, len(friends))

    def send(source, target, send_sem, recv_sem, where):
        copy = pltpu.make_async_remote_copy(
            src_ref=source, dst_ref=target, send_sem=send_sem, recv_sem=recv_sem,
            device_id=where, device_id_type=MESH,
        )
        copy.start()

    def arrived(ref, sem):
        pltpu.make_async_copy(ref, ref, sem).wait()

    plus = [device(shifted(spot, axis, 1), core) for axis in range(3)]
    minus = [device(shifted(spot, axis, 3), core) for axis in range(3)]
    plus_other = [device(shifted(spot, axis, 1), other) for axis in range(3)]
    minus_other = [device(shifted(spot, axis, 3), other) for axis in range(3)]

    def spread(k, d1):
        a2 = ORDERS[k][1]
        own = held[k][0].at[d1]
        send(own, held[k][3].at[d1], held_send.at[k], two_recv.at[k, d1, 0], plus[a2])
        send(own, held[k][1].at[d1], held_send.at[k], two_recv.at[k, d1, 1], minus[a2])

    def spread_on(k, d1):
        a2 = ORDERS[k][1]
        arrived(held[k][3].at[d1], two_recv.at[k, d1, 0])
        send(held[k][3].at[d1, 0:2], held[k][2].at[d1, 0:2], held_send.at[k], two_recv.at[k, d1, 2], plus[a2])
        arrived(held[k][1].at[d1], two_recv.at[k, d1, 1])
        send(held[k][1].at[d1, 2:4], held[k][2].at[d1, 2:4], held_send.at[k], two_recv.at[k, d1, 3], minus[a2])

    def part(k, source, d2):
        return outs[k].at[pl.ds(source * 16 + d2 * 4, 4)]

    def select(k, d2):
        a1, a2, a3 = ORDERS[k]
        for d1 in range(4):
            group, member = device(shifted(shifted(spot, a1, d1), a2, d2), core)
            lane = group * 64 + member
            for j in range(8):
                row = j if j < 2 else 2 + k * 6 + (j - 2)
                block = held[k][d2][d1, wants[row, 0, lane]]
                if j == 0:
                    outs[k][d2 * 4 + d1] = block
                else:
                    packs[k][j - 1, d2, d1] = block
        send(packs[k].at[0, d2], part(k, 1, d2), pack_send.at[k], out_recv.at[k], device(spot, other))
        send(packs[k].at[3, d2], relays[k].at[0, d2], pack_send.at[k], relay_recv.at[k, 0, d2], plus[a3])
        send(packs[k].at[4, d2], relays[k].at[1, d2], pack_send.at[k], relay_recv.at[k, 1, d2], minus[a3])
        send(packs[k].at[1, d2], part(k, 6, d2), pack_send.at[k], out_recv.at[k], plus[a3])
        send(packs[k].at[5, d2], part(k, 2, d2), pack_send.at[k], out_recv.at[k], minus[a3])
        send(packs[k].at[2, d2], part(k, 7, d2), pack_send.at[k], out_recv.at[k], plus_other[a3])
        send(packs[k].at[6, d2], part(k, 3, d2), pack_send.at[k], out_recv.at[k], minus_other[a3])

    def relay(k, d2):
        a3 = ORDERS[k][2]
        arrived(relays[k].at[0, d2], relay_recv.at[k, 0, d2])
        send(relays[k].at[0, d2], part(k, 4, d2), relay_send.at[k], out_recv.at[k], plus[a3])
        arrived(relays[k].at[1, d2], relay_recv.at[k, 1, d2])
        send(relays[k].at[1, d2], part(k, 5, d2), relay_send.at[k], out_recv.at[k], minus_other[a3])

    for k in range(3):
        loads[k].wait()
        a1 = ORDERS[k][0]
        own = held[k][0].at[0]
        send(own, held[k][0].at[3], held_send.at[k], one_recv.at[k, 0], plus[a1])
        send(own, held[k][0].at[1], held_send.at[k], one_recv.at[k, 1], minus[a1])
        spread(k, 0)
    late_loads = [
        load(feat, feat_vec, 6), load(deg_hbm, deg, 7), load(self_hbm, w_self, 8),
        load(neigh_hbm, w_neigh, 9), load(bias_hbm, bias, 10), load(tiles, tiles_vec, 11),
    ]
    for copy in table_loads:
        copy.wait()

    lanes = lax.broadcasted_iota(jnp.int32, (1, 128), 1)
    want = jnp.zeros((1, 128), jnp.int32)
    for b in range(4):
        for t in range(32):
            block = src[b, t]
            owner = jnp.where(t < cnt[b], lax.shift_right_logical(block, 2), -1)
            want = jnp.where(lanes == owner, lax.bitwise_and(block, 3), want)
    mine[...] = want
    send(mine, table.at[0], want_send, want_recv, device(spot, other))
    for k in range(3):
        a3 = ORDERS[k][2]
        for e in (1, 2, 3):
            back = shifted(spot, a3, 4 - e)
            send(mine, table.at[1 + k * 6 + e * 2 - 2], want_send, want_recv, device(back, core))
            send(mine, table.at[1 + k * 6 + e * 2 - 1], want_send, want_recv, device(back, other))

    owner = lax.shift_right_logical(src_vec[...], 2)
    rc = lax.bitwise_xor(lax.bitwise_and(owner, 1), core)
    sy = lax.bitwise_and(lax.shift_right_logical(owner, 1), 3)
    sx = lax.bitwise_and(lax.shift_right_logical(owner, 4), 3)
    sz = lax.bitwise_and(lax.shift_right_logical(owner, 3), 1) + 2 * lax.shift_right_logical(owner, 6)
    rx, ry, rz = (lax.bitwise_and(s - m, 3) for s, m in zip((sx, sy, sz), spot))
    slots = lax.broadcasted_iota(jnp.int32, (4, 32), 1)
    which = lax.broadcasted_iota(jnp.int32, (4, 32), 0)
    counts = jnp.where(which == 0, cnt[0], jnp.where(which == 1, cnt[1], jnp.where(which == 2, cnt[2], cnt[3])))
    for k, (d1, d2, d3) in enumerate(((rx, ry, rz), (ry, rz, rx), (rz, rx, ry))):
        spots_vec[k] = jnp.where(slots < counts, ((d3 * 2 + rc) * 4 + d2) * 4 + d1, 128)
    spots_copy = pltpu.make_async_copy(spots_vec, spots, want_local.at[2])
    spots_copy.start()
    for k, (_, rows) in enumerate(SPLITS):
        outs[k][128] = jnp.zeros((rows, 128), jnp.bfloat16)

    for k in range(3):
        a1 = ORDERS[k][0]
        arrived(held[k][0].at[3], one_recv.at[k, 0])
        send(held[k][0].at[3, 0:2], held[k][0].at[2, 0:2], held_send.at[k], one_recv.at[k, 2], plus[a1])
        spread(k, 3)
        arrived(held[k][0].at[1], one_recv.at[k, 1])
        send(held[k][0].at[1, 2:4], held[k][0].at[2, 2:4], held_send.at[k], one_recv.at[k, 3], minus[a1])
        spread(k, 1)
    for k in range(3):
        spread_on(k, 0)
    for k in range(3):
        arrived(held[k][0].at[2, 0:2], one_recv.at[k, 2])
        arrived(held[k][0].at[2, 2:4], one_recv.at[k, 3])
        spread(k, 2)

    arrived(table, want_recv)
    own_row = pltpu.make_async_copy(mine, wants.at[0], want_local.at[0])
    others = pltpu.make_async_copy(table, wants.at[pl.ds(1, 19)], want_local.at[1])
    own_row.start()
    others.start()
    own_row.wait()
    others.wait()

    for k in range(3):
        select(k, 0)
        spread_on(k, 3)
        spread_on(k, 1)
    for k in range(3):
        spread_on(k, 2)
        select(k, 3)
        select(k, 1)
        relay(k, 0)
    for k in range(3):
        for d1 in range(4):
            arrived(held[k][2].at[d1, 0:2], two_recv.at[k, d1, 2])
            arrived(held[k][2].at[d1, 2:4], two_recv.at[k, d1, 3])
        select(k, 2)
    for k in range(3):
        relay(k, 3)
        relay(k, 1)

    for copy in late_loads:
        copy.wait()
    for b in range(4):
        base[b] = jnp.dot(feat_vec[b], w_self[...], preferred_element_type=jnp.float32) + bias[...]

    for k in range(3):
        relay(k, 2)
    spots_copy.wait()
    for k in range(3):
        arrived(outs[k].at[pl.ds(16, 112)], out_recv.at[k])

    def one_block(b, carry):
        total = jnp.zeros((128, 128), jnp.float32)
        for pair in range(16):
            slot_pair = (2 * pair, 2 * pair + 1)
            blocks = [outs[k][spots[k, b, t]] for t in slot_pair for k in range(3)]
            total = total + jnp.dot(
                jnp.concatenate([tiles_vec[b, t] for t in slot_pair], axis=1),
                jnp.concatenate(blocks, axis=0),
                preferred_element_type=jnp.float32,
            )
        degrees = jnp.broadcast_to(deg[pl.ds(b, 1), :].astype(jnp.float32), (128, 128)).T
        mean = (total / degrees).astype(jnp.bfloat16)
        summed = base[b] + jnp.dot(mean, w_neigh[...], preferred_element_type=jnp.float32)
        out[b] = jnp.maximum(summed, 0.0).astype(jnp.bfloat16)
        return carry

    lax.fori_loop(0, 4, one_block, 0)

    arrived(table, want_send)
    for k in range(3):
        arrived(packs[k], pack_send.at[k])
        arrived(relays[k], relay_send.at[k])
        sent = packs[k].at[pl.ds(0, 3), pl.ds(0, 4), pl.ds(0, 4)]
        arrived(sent, held_send.at[k])
        more = packs[k].at[0, pl.ds(0, 3), pl.ds(0, 4)]
        arrived(more, held_send.at[k])


def per_device(features, tiles, tile_src, tile_count, degrees, w_self, w_neigh, bias):
    rows = [r for _, r in SPLITS]
    dma = pltpu.SemaphoreType.DMA
    wide, whole, real = jnp.bfloat16, jnp.int32, jnp.float32
    scratch = [pltpu.VMEM((4, 4, r, 128), wide) for r in rows for _ in range(4)]
    scratch += [pltpu.VMEM((7, 4, 4, r, 128), wide) for r in rows]
    scratch += [pltpu.VMEM((2, 4, 4, r, 128), wide) for r in rows]
    scratch += [pltpu.VMEM((129, r, 128), wide) for r in rows]
    scratch += [pltpu.VMEM((1, 128), whole), pltpu.VMEM((19, 1, 128), whole), pltpu.SMEM((20, 1, 128), whole)]
    scratch += [pltpu.SMEM((4, 32), whole), pltpu.SMEM((4,), whole), pltpu.VMEM((4, 32), whole)]
    scratch += [pltpu.VMEM((3, 4, 32), whole), pltpu.SMEM((3, 4, 32), whole)]
    scratch += [pltpu.VMEM((4, 128, 128), wide), pltpu.VMEM((4, 32, 128, 128), wide), pltpu.VMEM((4, 128), whole)]
    scratch += [pltpu.VMEM((128, 128), wide), pltpu.VMEM((128, 128), wide), pltpu.VMEM((1, 128), real)]
    scratch += [pltpu.VMEM((4, 128, 128), real)]
    scratch += [dma((12,)), dma((3, 4)), dma((3, 4, 4)), dma((3,))]
    scratch += [dma, dma, dma((3,)), dma((3,)), dma((3,)), dma((3, 2, 4)), dma((3,))]
    updated = pl.pallas_call(
        layer_kernel,
        out_shape=pltpu.VMEM((4, 128, 128), jnp.bfloat16),
        in_specs=[pl.BlockSpec(memory_space=pl.ANY)] * 8,
        out_specs=pl.BlockSpec(memory_space=pltpu.VMEM),
        scratch_shapes=scratch,
        compiler_params=pltpu.CompilerParams(
            collective_id=0, has_side_effects=True, vmem_limit_bytes=VMEM_BYTES
        ),
        name="layer",
    )(
        features.reshape(4, 128, 128), tiles, tile_src, tile_count,
        degrees.reshape(4, 128), w_self, w_neigh, bias.reshape(1, 128),
    )
    return updated.reshape(features.shape)


def solution(mesh):
    return jax.shard_map(
        per_device,
        mesh=mesh,
        in_specs=(
            P(("blk", "row"), None),
            P(("blk", "row"), None, None, None),
            P(("blk", "row"), None),
            P(("blk", "row")),
            P(("blk", "row")),
            P(),
            P(),
            P(),
        ),
        out_specs=P(("blk", "row"), None),
        check_vma=False,
    )
```

```python
import jax
import jax.numpy as jnp
from jax import lax
from jax.experimental import pallas as pl
from jax.experimental.pallas import tpu as pltpu
from jax.sharding import PartitionSpec as P

MESH = pl.DeviceIdType.MESH
VMEM_BYTES = 66_800_000
COLOURS = ((0, 48, (0, 1, 2), 0), (48, 48, (1, 2, 0), 1), (96, 32, (2, 0, 1), 0))
INNER = (
    ((0, 0, 0), -1, 0),
    ((1, 0, 0), 0, 1),
    ((0, 1, 0), 0, 1),
    ((0, 0, 3), 0, 1),
    ((1, 3, 0), 1, 2),
    ((1, 0, 3), 1, 2),
    ((3, 1, 0), 2, 2),
    ((0, 1, 1), 2, 2),
    ((0, 3, 3), 3, 2),
    ((2, 3, 0), 4, 3),
    ((1, 1, 3), 5, 3),
    ((1, 0, 2), 5, 3),
    ((3, 1, 1), 7, 3),
    ((0, 2, 1), 7, 3),
    ((2, 3, 1), 9, 4),
    ((1, 2, 3), 10, 4),
    ((3, 1, 2), 12, 4),
    ((3, 2, 2), 16, 5),
)
LEAVES = (
    ((0, 3, 0), 0), ((3, 0, 0), 0), ((0, 0, 1), 0), ((2, 0, 0), 1),
    ((1, 0, 1), 1), ((0, 1, 3), 2), ((1, 1, 0), 2), ((0, 2, 0), 2),
    ((3, 0, 3), 3), ((0, 0, 2), 3), ((1, 2, 0), 4), ((1, 3, 3), 4),
    ((1, 3, 1), 4), ((2, 0, 3), 5), ((2, 1, 0), 6), ((3, 2, 0), 6),
    ((3, 1, 3), 6), ((1, 1, 1), 7), ((0, 1, 2), 7), ((3, 3, 3), 8),
    ((0, 2, 3), 8), ((0, 3, 2), 8), ((2, 2, 0), 9), ((3, 3, 0), 9),
    ((2, 3, 3), 9), ((2, 1, 3), 10), ((1, 1, 2), 10), ((1, 3, 2), 11),
    ((2, 0, 2), 11), ((2, 1, 1), 12), ((3, 0, 1), 12), ((0, 3, 1), 13),
    ((1, 2, 1), 13), ((3, 2, 1), 13), ((0, 2, 2), 13), ((2, 2, 1), 14),
    ((2, 0, 1), 14), ((3, 3, 1), 14), ((2, 3, 2), 14), ((2, 2, 3), 15),
    ((1, 2, 2), 15), ((3, 0, 2), 16), ((2, 1, 2), 16), ((3, 2, 3), 17),
    ((3, 3, 2), 17), ((2, 2, 2), 17),
)
HELD = len(INNER)
PICKED = 128 - HELD


def place():
    group, member = lax.axis_index("blk"), lax.axis_index("row")
    x = lax.div(member, 16)
    z_low = lax.rem(lax.div(member, 8), 2)
    y = lax.rem(lax.div(member, 2), 4)
    return [x, y, group * 2 + z_low], lax.rem(member, 2)


def device(spot, core):
    x, y, z = spot
    return lax.div(z, 2), ((x * 2 + lax.rem(z, 2)) * 4 + y) * 2 + core


def either(flip, first, second):
    same = isinstance(first, int) and first == second
    return first if same else first + flip * (second - first)


def edge(offset, parent):
    from_parent = [(o - p) % 4 for o, p in zip(offset, INNER[parent][0])]
    axis = [a for a in range(3) if from_parent[a]][0]
    return axis, from_parent[axis] // 2


def layer_kernel(feat, tiles, src_hbm, cnt_hbm, deg_hbm, self_hbm, neigh_hbm, bias_hbm, out, *scratch):
    colours = range(len(COLOURS))
    refs = list(scratch)
    held = [[refs.pop(0) for _ in range(HELD)] for _ in colours]
    packs = [refs.pop(0) for _ in colours]
    picked, mine, table, wants, src, cnt, src_vec, spots_vec, spots = refs[:9]
    feat_vec, tiles_vec, deg, w_self, w_neigh, bias, base = refs[9:16]
    load_sem, held_recv, held_send, want_send, want_recv, want_local, pack_send, picked_recv = refs[16:]

    spot, core = place()
    other = 1 - core

    def load(source, target, at):
        copy = pltpu.make_async_copy(source, target, load_sem.at[at])
        copy.start()
        return copy

    own_loads = [
        load(feat.at[:, pl.ds(COLOURS[k][0], COLOURS[k][1]), :], held[k][0], 9 + k) for k in colours
    ]
    table_loads = [load(src_hbm, src, 0), load(cnt_hbm, cnt, 1), load(src_hbm, src_vec, 2)]

    near = {}
    for axis in range(3):
        for down in (0, 1):
            moved = list(spot)
            moved[axis] = lax.rem(moved[axis] + (3 if down else 1), 4)
            for c, at in enumerate((core, other)):
                near[axis, down, c] = device(moved, at)
    partner = device(spot, other)
    friends = [partner] + list(near.values())
    barrier = pltpu.get_barrier_semaphore()
    for friend in friends:
        pl.semaphore_signal(barrier, inc=1, device_id=friend, device_id_type=MESH)
    pl.semaphore_wait(barrier, len(friends))

    def send(source, target, send_sem, recv_sem, where):
        pltpu.make_async_remote_copy(
            src_ref=source, dst_ref=target, send_sem=send_sem, recv_sem=recv_sem,
            device_id=where, device_id_type=MESH,
        ).start()

    def arrived(ref, sem):
        pltpu.make_async_copy(ref, ref, sem).wait()

    flips = [core if mirror == 0 else other for _, _, _, mirror in COLOURS]

    def toward(k, axis, down, c):
        real = COLOURS[k][2][axis]
        up, low = near[real, down, c], near[real, 1 - down, c]
        return either(flips[k], up[0], low[0]), either(flips[k], up[1], low[1])

    def laid(k, offset):
        real = [0, 0, 0]
        for axis in range(3):
            real[COLOURS[k][2][axis]] = offset[axis]
        return real

    def number(k, offset, c):
        x, y, z = laid(k, offset)
        mx, my, mz = (-x % 4, -y % 4, -z % 4)
        return either(flips[k], ((x * 4 + y) * 4 + z) * 2 + c, ((mx * 4 + my) * 4 + mz) * 2 + c)

    lane_parts = {}

    def lane_part(k, axis, step):
        key = (COLOURS[k][3], axis, step)
        if key not in lane_parts:
            at = lax.rem(spot[axis] + either(flips[k], -step % 4, step), 4)
            lane_parts[key] = (
                at * 16 if axis == 0 else at * 2 if axis == 1 else lax.div(at, 2) * 64 + lax.rem(at, 2) * 8
            )
        return lane_parts[key]

    def pass_on(k, i):
        for j, (offset, parent, _) in enumerate(INNER):
            if parent == i:
                send(held[k][i], held[k][j], held_send.at[k], held_recv.at[k, j], toward(k, *edge(offset, i), 0))

    waiting = []

    def flush():
        for args in waiting:
            send(*args)
        waiting.clear()

    def select(k, i):
        start, rows = COLOURS[k][:2]
        mine_offset = INNER[i][0]
        steps = laid(k, mine_offset)
        lane = lane_part(k, 0, steps[0]) + lane_part(k, 1, steps[1]) + lane_part(k, 2, steps[2]) + core
        picked[number(k, mine_offset, 0), pl.ds(start, rows), :] = held[k][i][wants[0, 0, lane]]
        packs[k][i] = held[k][i][wants[1, 0, lane]]
        sends = [(i, mine_offset, 1, partner)]
        for l, (offset, parent) in enumerate(LEAVES):
            if parent != i:
                continue
            axis, down = edge(offset, i)
            real = COLOURS[k][2][axis]
            for c in (0, 1):
                row = 2 + (real * 2 + either(flips[k], down, 1 - down)) * 2 + c
                at = HELD + 2 * l + c
                packs[k][at] = held[k][i][wants[row, 0, lane]]
                sends.append((at, offset, c, toward(k, axis, down, c)))
        flush()
        for at, offset, c, where in sends:
            target = picked.at[number(k, offset, c), pl.ds(start, rows), :]
            waiting.append((packs[k].at[at], target, pack_send.at[k], picked_recv.at[k], where))

    for k in colours:
        own_loads[k].wait()
        pass_on(k, 0)
    late_loads = [
        load(feat, feat_vec, 3), load(deg_hbm, deg, 4), load(self_hbm, w_self, 5),
        load(neigh_hbm, w_neigh, 6), load(bias_hbm, bias, 7), load(tiles, tiles_vec, 8),
    ]
    for copy in table_loads:
        copy.wait()

    lanes = lax.broadcasted_iota(jnp.int32, (1, 128), 1)
    want = jnp.zeros((1, 128), jnp.int32)
    for b in range(4):
        for t in range(32):
            block = src[b, t]
            owner = jnp.where(t < cnt[b], lax.shift_right_logical(block, 2), -1)
            want = jnp.where(lanes == owner, lax.bitwise_and(block, 3), want)
    mine[...] = want

    owner = lax.shift_right_logical(src_vec[...], 2)
    rc = lax.bitwise_xor(lax.bitwise_and(owner, 1), core)
    sy = lax.bitwise_and(lax.shift_right_logical(owner, 1), 3)
    sx = lax.bitwise_and(lax.shift_right_logical(owner, 4), 3)
    sz = lax.bitwise_and(lax.shift_right_logical(owner, 3), 1) + 2 * lax.shift_right_logical(owner, 6)
    vx, vy, vz = (lax.bitwise_and(m - s, 3) for s, m in zip((sx, sy, sz), spot))
    slots = lax.broadcasted_iota(jnp.int32, (4, 32), 1)
    which = lax.broadcasted_iota(jnp.int32, (4, 32), 0)
    counts = jnp.where(which == 0, cnt[0], jnp.where(which == 1, cnt[1], jnp.where(which == 2, cnt[2], cnt[3])))
    spots_vec[...] = jnp.where(slots < counts, ((vx * 4 + vy) * 4 + vz) * 2 + rc, 128)

    send(mine, table.at[0], want_send, want_recv, partner)
    for (axis, down, c), where in near.items():
        send(mine, table.at[1 + (axis * 2 + 1 - down) * 2 + c], want_send, want_recv, where)
    spots_copy = pltpu.make_async_copy(spots_vec, spots, want_local.at[2])
    spots_copy.start()
    own_row = pltpu.make_async_copy(mine, wants.at[0], want_local.at[0])
    own_row.start()
    picked[128] = jnp.zeros((128, 128), jnp.bfloat16)

    levels = [[i for i, node in enumerate(INNER) if node[2] == level] for level in range(INNER[-1][2] + 1)]

    def step(level):
        for i in levels[level]:
            for k in colours:
                arrived(held[k][i], held_recv.at[k, i])
                pass_on(k, i)

    step(1)
    arrived(table, want_recv)
    others = pltpu.make_async_copy(table, wants.at[pl.ds(1, 13)], want_local.at[1])
    others.start()
    own_row.wait()
    others.wait()
    for k in colours:
        select(k, 0)
    for level in range(1, len(levels)):
        for i in levels[level]:
            for k in colours:
                select(k, i)
        flush()
        if level + 1 < len(levels):
            step(level + 1)

    for copy in late_loads:
        copy.wait()
    for b in range(4):
        base[b] = jnp.dot(feat_vec[b], w_self[...], preferred_element_type=jnp.float32) + bias[...]
    spots_copy.wait()
    for k in colours:
        start, rows = COLOURS[k][:2]
        arrived(picked.at[pl.ds(0, PICKED), pl.ds(start, rows), :], picked_recv.at[k])

    def one_block(b, carry):
        total = jnp.zeros((128, 128), jnp.float32)
        for pair in range(16):
            slot_pair = (2 * pair, 2 * pair + 1)
            total = total + jnp.dot(
                jnp.concatenate([tiles_vec[b, t] for t in slot_pair], axis=1),
                jnp.concatenate([picked[spots[b, t]] for t in slot_pair], axis=0),
                preferred_element_type=jnp.float32,
            )
        degrees = jnp.broadcast_to(deg[pl.ds(b, 1), :].astype(jnp.float32), (128, 128)).T
        mean = (total / degrees).astype(jnp.bfloat16)
        summed = base[b] + jnp.dot(mean, w_neigh[...], preferred_element_type=jnp.float32)
        out[b] = jnp.maximum(summed, 0.0).astype(jnp.bfloat16)
        return carry

    lax.fori_loop(0, 4, one_block, 0)

    arrived(table, want_send)
    for k in colours:
        start, rows = COLOURS[k][:2]
        arrived(packs[k], pack_send.at[k])
        arrived(picked.at[pl.ds(0, 4 * (HELD - 1)), pl.ds(start, rows), :], held_send.at[k])


def per_device(features, tiles, tile_src, tile_count, degrees, w_self, w_neigh, bias):
    rows = [colour[1] for colour in COLOURS]
    n = len(rows)
    dma = pltpu.SemaphoreType.DMA
    wide, whole, real = jnp.bfloat16, jnp.int32, jnp.float32
    scratch = [pltpu.VMEM((4, r, 128), wide) for r in rows for _ in range(HELD)]
    scratch += [pltpu.VMEM((HELD + 2 * len(LEAVES), r, 128), wide) for r in rows]
    scratch += [pltpu.VMEM((129, 128, 128), wide)]
    scratch += [pltpu.VMEM((1, 128), whole), pltpu.VMEM((13, 1, 128), whole), pltpu.SMEM((14, 1, 128), whole)]
    scratch += [pltpu.SMEM((4, 32), whole), pltpu.SMEM((4,), whole), pltpu.VMEM((4, 32), whole)]
    scratch += [pltpu.VMEM((4, 32), whole), pltpu.SMEM((4, 32), whole)]
    scratch += [pltpu.VMEM((4, 128, 128), wide), pltpu.VMEM((4, 32, 128, 128), wide), pltpu.VMEM((4, 128), whole)]
    scratch += [pltpu.VMEM((128, 128), wide), pltpu.VMEM((128, 128), wide), pltpu.VMEM((1, 128), real)]
    scratch += [pltpu.VMEM((4, 128, 128), real)]
    scratch += [dma((9 + n,)), dma((n, HELD)), dma((n,)), dma, dma, dma((3,)), dma((n,)), dma((n,))]
    updated = pl.pallas_call(
        layer_kernel,
        out_shape=pltpu.VMEM((4, 128, 128), jnp.bfloat16),
        in_specs=[pl.BlockSpec(memory_space=pl.ANY)] * 8,
        out_specs=pl.BlockSpec(memory_space=pltpu.VMEM),
        scratch_shapes=scratch,
        compiler_params=pltpu.CompilerParams(
            collective_id=0, has_side_effects=True, vmem_limit_bytes=VMEM_BYTES
        ),
        name="layer",
    )(
        features.reshape(4, 128, 128), tiles, tile_src, tile_count,
        degrees.reshape(4, 128), w_self, w_neigh, bias.reshape(1, 128),
    )
    return updated.reshape(features.shape)


def solution(mesh):
    return jax.shard_map(
        per_device,
        mesh=mesh,
        in_specs=(
            P(("blk", "row"), None),
            P(("blk", "row"), None, None, None),
            P(("blk", "row"), None),
            P(("blk", "row")),
            P(("blk", "row")),
            P(),
            P(),
            P(),
        ),
        out_specs=P(("blk", "row"), None),
        check_vma=False,
    )
```
